512 devices in a mesh: chan: 8 (over y, x_lo), tile: 64 (over z, x_hi, core).
Axes of the slice: x: 4 (x_hi: 2, x_lo: 2; x = x_hi * 2 + x_lo), y: 4, z: 16, core: 2. Of those that a mesh axis runs over, the one named last changes fastest.
Arguments:
- image: bfloat16 [256, 1024, 256], P('chan', 'tile'), may hold values from -6 to 6
- w_down: bfloat16 [2, 2, 256, 512], P(None, None, None, 'chan'), may hold values from -0.1875 to 0.1875
- w_mix: bfloat16 [3, 3, 512, 512], P(None, None, None, 'chan'), may hold values from -0.09375 to 0.09375
- cotangent: bfloat16 [512, 512, 128], P('chan', 'tile'), may hold values from -6 to 6
Outputs:
- mixed: bfloat16 [512, 512, 128], P('chan', 'tile')
- grad_mix: float32 [512, 3, 3, 512], P('tile', None, None, 'chan')
- grad_down: float32 [256, 2, 2, 512], P('tile', None, None, 'chan')
- grad_image: bfloat16 [256, 1024, 256], P('chan', 'tile')
The draws below stay inside these ranges and needn't reach their ends.
All inputs are finite; a program needn't handle non-finite values.
Results may differ from the reference program's by a relative error of at most 0.0049.
Values may be sent and summed in bfloat16 or wider, within the bound.
No kernel may reach another device: no remote copies, remote signals or barrier semaphores. Data moves between devices by JAX's collectives and lax.ppermute only.
A program may use at most 64 MiB of HBM per device.

```python
import math
import jax
import jax.numpy as jnp

C0 = 256
C1 = 512
COLS = 128
OUT_ROWS = 512


def levels(own_key, dims, cuts, low, top_value):
    gain = 1.0
    for axis_at, shards_of in cuts:
        draws = jax.random.uniform(jax.random.fold_in(jax.random.fold_in(own_key, 6), axis_at), (shards_of,), jnp.float32, low / len(cuts), top_value / len(cuts))
        gain = gain * jnp.repeat(jnp.exp(draws), dims[axis_at] // shards_of).reshape((-1,) + (1,) * (len(dims) - 1 - axis_at))
    return gain


def bell_draw(stream_key, extent, deviation, reach, cuts=(), held_as=jnp.bfloat16):
    gain = levels(stream_key, extent, cuts, -0.22, 0.18) if cuts else 1.0
    array = jax.random.normal(stream_key, extent, jnp.float32) * deviation * gain
    return jnp.minimum(jnp.maximum(array, -reach), reach).astype(held_as)


def setup_inputs(seed: int = 0) -> dict:
    key_of = jax.random.split(jax.random.key(seed), 5)
    image = bell_draw(key_of[0], (C0, 2 * OUT_ROWS, 2 * COLS), 1.0, 6.0, ((0, 8), (1, 64)))
    w_down = bell_draw(key_of[1], (2, 2, C0, C1), (4 * C0) ** -0.5, 0.1875, ((3, 8),))
    w_mix = bell_draw(key_of[2], (3, 3, C1, C1), (9 * C1) ** -0.5, 0.09375, ((3, 8),))
    cotangent = bell_draw(key_of[3], (C1, OUT_ROWS, COLS), 1.0, 6.0, ((0, 8), (1, 64)))
    return dict(image=image, w_down=w_down, w_mix=w_mix, cotangent=cotangent)


def normal_cdf(value):
    return 0.5 * (1.0 + jax.scipy.special.erf(value / math.sqrt(2.0)))

def normal_pdf(value):
    return jnp.exp(-0.5 * value * value) / math.sqrt(2.0 * math.pi)

def reference(image, w_down, w_mix, cotangent):
    in_chan, in_rows, in_cols = image.shape
    n_rows = in_rows // 2
    n_cols = in_cols // 2
    scale = 1.0 / math.sqrt(n_rows * n_cols)
    patches = image.astype(jnp.float32).reshape(in_chan, n_rows, 2, n_cols, 2)
    down32 = w_down.astype(jnp.float32)
    mix32 = w_mix.astype(jnp.float32)
    preact = jnp.einsum('crawb,abcd->drw', patches, down32)
    hidden = (preact * normal_cdf(preact)).astype(jnp.bfloat16)
    hidden_pad = jnp.pad(hidden.astype(jnp.float32), ((0, 0), (1, 1), (1, 1)))
    mixed = jnp.zeros(preact.shape, jnp.float32)
    for tap_row in range(3):
        for tap_col in range(3):
            window = hidden_pad[:, tap_row:tap_row + n_rows, tap_col:tap_col + n_cols]
            mixed = mixed + jnp.einsum('crw,cd->drw', window, mix32[tap_row, tap_col])
    cot32 = cotangent.astype(jnp.float32)
    cot_pad = jnp.pad(cot32, ((0, 0), (1, 1), (1, 1)))
    mix_terms = []
    grad_hidden = jnp.zeros(preact.shape, jnp.float32)
    for tap_row in range(3):
        for tap_col in range(3):
            window = hidden_pad[:, tap_row:tap_row + n_rows, tap_col:tap_col + n_cols]
            mix_terms.append(jnp.einsum('crw,drw->cd', window, cot32))
            back = cot_pad[:, 2 - tap_row:2 - tap_row + n_rows, 2 - tap_col:2 - tap_col + n_cols]
            grad_hidden = grad_hidden + jnp.einsum('drw,cd->crw', back, mix32[tap_row, tap_col])
    grad_mix = jnp.stack(mix_terms, 1).reshape(mix32.shape[2], 3, 3, mix32.shape[3]) * scale
    slope = normal_cdf(preact) + preact * normal_pdf(preact)
    grad_pre = (grad_hidden * slope).astype(jnp.bfloat16).astype(jnp.float32)
    grad_down = jnp.einsum('crawb,drw->cabd', patches, grad_pre) * scale
    grad_image = jnp.einsum('drw,abcd->crawb', grad_pre, down32).reshape(in_chan, in_rows, in_cols)
    return (mixed.astype(jnp.bfloat16), grad_mix, grad_down, grad_image.astype(jnp.bfloat16))
```

```python
import math

import jax
import jax.numpy as jnp
from jax import lax
from jax.experimental import pallas as pl
from jax.experimental.pallas import tpu as pltpu
from jax.sharding import Mesh, PartitionSpec as P

TILE = ("z", "xh", "core")
BF16 = jnp.bfloat16
F32 = jnp.float32


def normal_cdf(value):
    return 0.5 * (1.0 + jax.scipy.special.erf(value / math.sqrt(2.0)))


def normal_pdf(value):
    return jnp.exp(-0.5 * value * value) / math.sqrt(2.0 * math.pi)


def dot(spec, left, right):
    return jnp.einsum(spec, left, right, preferred_element_type=F32)


def swap(block, axis):
    return lax.all_to_all(block, axis, 0, 0)


def spread(block):
    count = lax.axis_size("chan")
    return swap(jnp.broadcast_to(block[None], (count,) + block.shape), "chan")


def halved(block, axis):
    mine = lax.axis_index(axis)
    keep = lax.dynamic_index_in_dim(block, mine, 0, keepdims=False)
    give = lax.dynamic_index_in_dim(block, 1 - mine, 0, keepdims=False).astype(BF16)
    return keep + lax.ppermute(give, axis, [(0, 1), (1, 0)]).astype(F32)


def mixed_kernel(mix_ref, hidden_ref, inner_ref, up_ref, down_ref):
    n_rows, _, n_cols = hidden_ref.shape
    own_out = inner_ref.shape[1]
    column = lax.broadcasted_iota(jnp.int32, (3, own_out, n_cols), 2)
    sums = [jnp.zeros((own_out, n_cols), F32) for _ in range(n_rows + 2)]
    for row in range(n_rows):
        heap = jnp.dot(mix_ref[...], hidden_ref[row], preferred_element_type=F32)
        heap = heap.reshape(3, 3, own_out, n_cols)
        left = jnp.where(column > 0, pltpu.roll(heap[:, 0], 1, 2), 0.0)
        right = jnp.where(column < n_cols - 1, pltpu.roll(heap[:, 2], n_cols - 1, 2), 0.0)
        line = left + heap[:, 1] + right
        for tap_row in range(3):
            sums[row + 2 - tap_row] = sums[row + 2 - tap_row] + line[tap_row]
    up_ref[...] = sums[0]
    down_ref[...] = sums[n_rows + 1]
    for row in range(n_rows):
        inner_ref[row] = sums[row + 1]


def mixed_parts(mix, hidden):
    n_rows, _, n_cols = hidden.shape
    own_out = mix.shape[0] // 9
    whole = pl.BlockSpec(memory_space=pltpu.VMEM)
    edge = jax.ShapeDtypeStruct((own_out, n_cols), F32)
    return pl.pallas_call(
        mixed_kernel,
        out_shape=(jax.ShapeDtypeStruct((n_rows, own_out, n_cols), F32), edge, edge),
        in_specs=[whole, whole],
        out_specs=(whole, whole, whole),
        cost_estimate=pl.CostEstimate(
            flops=2 * mix.size * n_rows * n_cols,
            bytes_accessed=2 * (mix.size + hidden.size) + 4 * n_rows * own_out * n_cols,
            transcendentals=0,
        ),
        compiler_params=pltpu.CompilerParams(vmem_limit_bytes=32 << 20),
    )(mix, hidden)


def per_device(image, w_down, w_mix, cotangent):
    n_chan = lax.axis_size("chan")
    n_tile = lax.axis_size(TILE)
    own_in, _, in_cols = image.shape
    own_out, n_rows, n_cols = cotangent.shape
    all_out = n_chan * own_out
    taps = 4 * own_in
    scale = 1.0 / math.sqrt(n_rows * n_tile * n_cols)
    chan = lax.axis_index("chan")
    ahead = [(i, i + 1) for i in range(n_tile - 1)]
    back = [(i + 1, i) for i in range(n_tile - 1)]

    cot = jnp.transpose(cotangent, (1, 0, 2))
    above = lax.ppermute(cot[n_rows - 1 :], TILE, ahead)
    below = lax.ppermute(cot[:1], TILE, back)
    rim = jnp.concatenate([above, cot, below], axis=0)
    rim = jnp.pad(rim, ((0, 0), (0, 0), (1, 1)))
    shifted = jnp.stack([rim[:, :, 2 - j : 2 - j + n_cols] for j in range(3)], axis=1)
    cols = jnp.stack(
        [
            jnp.concatenate([shifted[r + 2 - i] for i in range(3)]).reshape(9 * own_out, n_cols)
            for r in range(n_rows)
        ]
    )

    mix = jnp.transpose(w_mix, (0, 1, 3, 2)).reshape(9 * own_out, all_out)

    even_odd = (
        jnp.arange(in_cols)[:, None, None]
        == 2 * jnp.arange(n_cols)[None, None, :] + jnp.arange(2)[None, :, None]
    ).astype(BF16)
    own_patches = dot("crax,xbw->rcabw", image.reshape(own_in, n_rows, 2, in_cols), even_odd)
    own_patches = own_patches.astype(BF16).reshape(n_rows, taps, n_cols)
    down = w_down.reshape(2, 2, n_chan, own_in, own_out)
    down = jnp.transpose(down, (2, 4, 3, 0, 1)).reshape(n_chan * own_out, taps)

    sent = jnp.concatenate(
        [jnp.broadcast_to(down[None], (n_chan,) + down.shape), own_patches], axis=1
    )
    partial = dot("kc,rkw->rcw", mix, cols).astype(BF16)
    got, partial = lax.optimization_barrier((swap(sent, "chan"), partial))
    all_down = got[:, : n_chan * own_out].reshape(n_chan, n_chan, own_out, taps)
    patches = got[:, n_chan * own_out :]
    preact = dot("sjdk,jkw->sdw", all_down, patches).reshape(all_out, n_cols)
    cdf = normal_cdf(preact)
    hidden = spread((preact * cdf).astype(BF16))

    grad_hidden = jnp.sum(swap(partial, "chan").astype(F32), axis=0)
    slope = cdf + preact * normal_pdf(preact)
    grad_pre = spread((grad_hidden * slope).astype(BF16))

    n_z, n_xh, n_core = (lax.axis_size(a) for a in TILE)
    rows = all_out // n_tile
    grad_mix = dot("rcw,rkw->ck", hidden, cols).reshape(n_z, n_xh, n_core, rows, 9 * own_out)
    grad_mix = halved(jnp.transpose(grad_mix, (2, 1, 0, 3, 4)), "core")
    grad_mix = halved(grad_mix, "xh")

    inner, up, down = mixed_parts(mix, hidden)
    from_below = lax.ppermute(up, TILE, back)
    from_above = lax.ppermute(down, TILE, ahead)
    edges = jnp.zeros_like(inner).at[0].set(from_above).at[n_rows - 1].set(from_below)
    mixed = jnp.transpose((inner + edges).astype(BF16), (1, 0, 2))

    grad_down = dot("rkw,rdw->kd", own_patches, grad_pre)
    groups = n_tile // n_chan
    lanes = 2 * own_out
    lines_of = taps * own_out // groups // lanes
    grad_down = grad_down.reshape(groups, 2, lines_of, n_chan, own_out)
    grad_down = jnp.transpose(grad_down, (0, 3, 2, 1, 4))
    grad_down = grad_down.reshape(n_z, n_xh, n_core, lines_of, lanes)
    grad_down = halved(jnp.transpose(grad_down, (2, 1, 0, 3, 4)), "core")
    grad_down = halved(grad_down, "xh")
    total = jnp.concatenate([grad_mix, grad_down], axis=-1).astype(BF16)
    total = jnp.sum(swap(total, "z").astype(F32), axis=0) * scale
    grad_mix = total[:, : 9 * own_out].reshape(rows, 3, 3, own_out)
    piece = total[:, 9 * own_out :]
    perm = [
        (k * n_tile + g * n_chan + to, to * n_tile + k * groups + g)
        for k in range(n_chan)
        for g in range(groups)
        for to in range(n_chan)
    ]
    piece = lax.ppermute(piece, ("chan",) + TILE, perm)
    grad_down = jnp.transpose(piece.reshape(lines_of, 2, own_out), (1, 0, 2))
    grad_down = grad_down.reshape(taps // groups // 4, 2, 2, own_out)

    turned = lax.dynamic_index_in_dim(all_down, chan, 1, keepdims=False).reshape(all_out, taps)
    grad_image = dot("dk,rdw->rkw", turned, grad_pre).astype(BF16)
    grad_image = dot(
        "rcabw,xbw->crax", grad_image.reshape(n_rows, own_in, 2, 2, n_cols), even_odd
    )
    grad_image = grad_image.astype(BF16).reshape(image.shape)
    return (mixed, grad_mix, grad_down, grad_image)


def solution(mesh):
    grid = mesh.devices
    n_chan, n_tile = grid.shape
    split = Mesh(grid.reshape(n_chan, n_tile // 4, 2, 2), ("chan",) + TILE)
    return jax.shard_map(
        per_device,
        mesh=split,
        in_specs=(
            P("chan", TILE, None),
            P(None, None, None, "chan"),
            P(None, None, None, "chan"),
            P("chan", TILE, None),
        ),
        out_specs=(
            P("chan", TILE, None),
            P(TILE, None, None, "chan"),
            P(TILE, None, None, "chan"),
            P("chan", TILE, None),
        ),
        check_vma=False,
    )
```

```python
import math

import jax
import jax.numpy as jnp
from jax import lax
from jax.experimental import pallas as pl
from jax.experimental.pallas import tpu as pltpu
from jax.sharding import Mesh, PartitionSpec as P

TILE = ("z", "xh", "core")
BF16 = jnp.bfloat16
F32 = jnp.float32


def normal_cdf(value):
    return 0.5 * (1.0 + jax.scipy.special.erf(value / math.sqrt(2.0)))


def normal_pdf(value):
    return jnp.exp(-0.5 * value * value) / math.sqrt(2.0 * math.pi)


def dot(spec, left, right):
    return jnp.einsum(spec, left, right, preferred_element_type=F32)


def swap(block, axis):
    return lax.all_to_all(block, axis, 0, 0)


def spread(block):
    count = lax.axis_size("chan")
    return swap(jnp.broadcast_to(block[None], (count,) + block.shape), "chan")


def halved(block, axis, dim):
    mine = lax.axis_index(axis)
    keep = lax.dynamic_index_in_dim(block, mine, dim, keepdims=False)
    give = lax.dynamic_index_in_dim(block, 1 - mine, dim, keepdims=False).astype(BF16)
    return keep + lax.ppermute(give, axis, [(0, 1), (1, 0)]).astype(F32)


def mixed_kernel(mix_ref, hidden_ref, inner_ref, up_ref, down_ref):
    own_out, cells = inner_ref.shape
    n_cols = up_ref.shape[1]
    column = lax.rem(lax.broadcasted_iota(jnp.int32, (own_out, cells), 1), n_cols)
    lines = []
    for tap_row in range(3):
        first = 3 * own_out * tap_row
        heap = jnp.dot(
            mix_ref[first : first + 3 * own_out, :], hidden_ref[...], preferred_element_type=F32
        )
        left = pltpu.roll(heap[:own_out], 1, 1)
        right = pltpu.roll(heap[2 * own_out :], cells - 1, 1)
        lines.append(
            jnp.where(column > 0, left, 0.0)
            + heap[own_out : 2 * own_out]
            + jnp.where(column < n_cols - 1, right, 0.0)
        )
    inner_ref[...] = lines[1]
    inner_ref[:, n_cols:] += lines[0][:, : cells - n_cols]
    inner_ref[:, : cells - n_cols] += lines[2][:, n_cols:]
    down_ref[...] = lines[0][:, cells - n_cols :]
    up_ref[...] = lines[2][:, :n_cols]


def mixed_parts(mix, hidden, n_cols):
    cells = hidden.shape[1]
    own_out = mix.shape[0] // 9
    whole = pl.BlockSpec(memory_space=pltpu.VMEM)
    edge = jax.ShapeDtypeStruct((own_out, n_cols), F32)
    return pl.pallas_call(
        mixed_kernel,
        out_shape=(jax.ShapeDtypeStruct((own_out, cells), F32), edge, edge),
        in_specs=[whole, whole],
        out_specs=(whole, whole, whole),
        cost_estimate=pl.CostEstimate(
            flops=2 * mix.size * cells,
            bytes_accessed=2 * (mix.size + hidden.size) + 4 * own_out * cells,
            transcendentals=0,
        ),
        compiler_params=pltpu.CompilerParams(vmem_limit_bytes=32 << 20),
    )(mix, hidden)


def per_device(image, w_down, w_mix, cotangent):
    n_chan = lax.axis_size("chan")
    n_z, n_xh, n_core = (lax.axis_size(a) for a in TILE)
    n_tile = n_z * n_xh * n_core
    own_in, _, in_cols = image.shape
    own_out, n_rows, n_cols = cotangent.shape
    cells = n_rows * n_cols
    all_in = n_chan * own_in
    all_out = n_chan * own_out
    taps = 4 * own_in
    scale = 1.0 / math.sqrt(cells * n_tile)
    ahead = [(i, i + 1) for i in range(n_tile - 1)]
    back = [(i + 1, i) for i in range(n_tile - 1)]

    even_odd = (
        jnp.arange(in_cols)[:, None, None]
        == 2 * jnp.arange(n_cols)[None, None, :] + jnp.arange(2)[None, :, None]
    ).astype(BF16)
    own_patches = dot("crax,xbw->rabcw", image.reshape(own_in, n_rows, 2, in_cols), even_odd)
    own_patches = jnp.transpose(own_patches.astype(BF16), (1, 2, 3, 0, 4)).reshape(taps, cells)
    own_patches, cotangent = lax.optimization_barrier((own_patches, cotangent))
    patches = spread(own_patches)

    above = lax.ppermute(cotangent[:, n_rows - 1], TILE, ahead)
    below = lax.ppermute(cotangent[:, 0], TILE, back)
    rim = jnp.concatenate([above, cotangent.reshape(own_out, cells), below], axis=1)
    rim = rim.reshape(own_out, n_rows + 2, n_cols)
    rim = jnp.pad(rim, ((0, 0), (0, 0), (1, 1)))
    cols = jnp.concatenate(
        [
            rim[:, 2 - i : 2 - i + n_rows, 2 - j : 2 - j + n_cols].reshape(own_out, cells)
            for i in range(3)
            for j in range(3)
        ]
    )

    mix = jnp.transpose(w_mix, (0, 1, 3, 2)).reshape(9 * own_out, all_out)
    partial = dot("kc,kq->cq", mix, cols).astype(BF16).reshape(n_chan, own_out, cells)
    turned = w_down.reshape(2, 2, n_chan, own_in, own_out)
    turned = jnp.transpose(turned, (2, 4, 0, 1, 3)).reshape(n_chan, own_out, taps)
    spare = own_out * taps // cells
    turned = turned.reshape(n_chan, own_out // spare, spare, taps)
    turned = jnp.transpose(turned, (0, 2, 1, 3)).reshape(n_chan, spare, cells)
    partial = jnp.concatenate([partial, turned], axis=1)
    patches, partial = lax.optimization_barrier((patches, partial))
    partial = swap(partial, "chan")

    down = jnp.transpose(w_down.reshape(2, 2, n_chan, own_in, own_out), (4, 2, 0, 1, 3))
    down = down.reshape(own_out, 4 * all_in)
    patches = patches.reshape(4 * all_in, cells)
    preact = dot("dk,kq->dq", down, patches)
    cdf = normal_cdf(preact)
    hidden = (preact * cdf).astype(BF16)
    hidden, partial = lax.optimization_barrier((hidden, partial))
    hidden = spread(hidden).reshape(all_out, cells)

    grad_hidden = jnp.sum(partial[:, :own_out].astype(F32), axis=0)
    slope = cdf + preact * normal_pdf(preact)
    grad_pre = (grad_hidden * slope).astype(BF16)
    grad_down = dot("kq,dq->kd", patches, grad_pre)
    groups = n_tile // n_chan
    group = own_in // groups
    grad_down = grad_down.reshape(n_chan, 2, 2, groups, group, own_out)
    grad_down = jnp.transpose(grad_down, (0, 3, 2, 4, 1, 5)).reshape(n_tile, 2 * group, 2 * own_out)

    grad_pre, hidden = lax.optimization_barrier((grad_pre, hidden))
    all_pre = spread(grad_pre).reshape(all_out, cells)

    rows = all_out // n_tile
    grad_mix = dot("cq,kq->ck", hidden, cols).reshape(n_tile, rows, 9 * own_out)
    total = jnp.concatenate([grad_mix, grad_down], axis=-1)
    total = total.reshape(n_z, n_xh, n_core, rows, -1)
    total = halved(halved(total, "core", 2), "xh", 1).astype(BF16)
    total = jnp.sum(swap(total, "z").astype(F32), axis=0) * scale
    grad_mix = total[:, : 9 * own_out].reshape(rows, 3, 3, own_out)
    piece = total[:, 9 * own_out :].reshape(2, group, 2, own_out)
    grad_down = jnp.transpose(piece, (1, 2, 0, 3))

    inner, up, down_edge = mixed_parts(mix, hidden, n_cols)
    from_below = lax.ppermute(up, TILE, back)
    from_above = lax.ppermute(down_edge, TILE, ahead)
    edges = jnp.concatenate(
        [from_above, jnp.zeros((own_out, cells - 2 * n_cols), F32), from_below], axis=1
    )
    mixed = (inner + edges).astype(BF16).reshape(own_out, n_rows, n_cols)

    turned = partial[:, own_out:].reshape(n_chan, spare, own_out // spare, taps)
    turned = jnp.transpose(turned, (0, 2, 1, 3)).reshape(all_out, taps)
    grad_image = dot("dk,dq->kq", turned, all_pre).astype(BF16)
    grad_image = grad_image.reshape(2, 2, own_in, n_rows, n_cols)
    grad_image = dot("abcrw,xbw->crax", grad_image, even_odd)
    grad_image = grad_image.astype(BF16).reshape(image.shape)
    return (mixed, grad_mix, grad_down, grad_image)


def solution(mesh):
    grid = mesh.devices
    n_chan, n_tile = grid.shape
    split = Mesh(grid.reshape(n_chan, n_tile // 4, 2, 2), ("chan",) + TILE)
    return jax.shard_map(
        per_device,
        mesh=split,
        in_specs=(
            P("chan", TILE, None),
            P(None, None, None, "chan"),
            P(None, None, None, "chan"),
            P("chan", TILE, None),
        ),
        out_specs=(
            P("chan", TILE, None),
            P(TILE, None, None, "chan"),
            P(TILE, None, None, "chan"),
            P("chan", TILE, None),
        ),
        check_vma=False,
    )
```

```python
import math

import jax
import jax.numpy as jnp
from jax import lax
from jax.experimental import pallas as pl
from jax.experimental.pallas import tpu as pltpu
from jax.sharding import Mesh, PartitionSpec as P

CHAN = ("y", "xl")
TILE = ("z", "xh", "core")
BF16 = jnp.bfloat16
F32 = jnp.float32


def normal_cdf(value):
    return 0.5 * (1.0 + jax.scipy.special.erf(value / math.sqrt(2.0)))


def normal_pdf(value):
    return jnp.exp(-0.5 * value * value) / math.sqrt(2.0 * math.pi)


def dot(spec, left, right):
    return jnp.einsum(spec, left, right, preferred_element_type=F32)


def swap(block, axis):
    return lax.all_to_all(block, axis, 0, 0)


def halved(block, axis, dim):
    mine = lax.axis_index(axis)
    keep = lax.dynamic_index_in_dim(block, mine, dim, keepdims=False)
    give = lax.dynamic_index_in_dim(block, 1 - mine, dim, keepdims=False).astype(BF16)
    return keep + lax.ppermute(give, axis, [(0, 1), (1, 0)]).astype(F32)


def call(kernel, outs, flops, *args):
    whole = pl.BlockSpec(memory_space=pltpu.VMEM)
    moved = sum(a.size * a.dtype.itemsize for a in args + tuple(outs))
    return pl.pallas_call(
        kernel,
        out_shape=tuple(outs),
        in_specs=[whole] * len(args),
        out_specs=(whole,) * len(outs),
        cost_estimate=pl.CostEstimate(flops=flops, bytes_accessed=moved, transcendentals=0),
        compiler_params=pltpu.CompilerParams(vmem_limit_bytes=12 << 20),
    )(*args)


def shape(dims, dtype):
    return jax.ShapeDtypeStruct(dims, dtype)


def moved(block, step, n_cols):
    width = block.shape[1]
    column = lax.rem(lax.broadcasted_iota(jnp.int32, block.shape, 1), n_cols)
    if step > 0:
        return jnp.where(column > 0, pltpu.roll(block, 1, 1), 0.0)
    return jnp.where(column < n_cols - 1, pltpu.roll(block, width - 1, 1), 0.0)


def grad_hidden_kernel(
    above_hbm, cot_hbm, below_hbm, mix_hbm, turned_hbm, cols_ref, out_hbm, rim_ref, mix_ref,
    part_ref, sems,
):
    own_out, n_cols = above_hbm.shape
    cells = cot_hbm.shape[1]
    n_chan, pair_out, half = part_ref.shape
    n_half = cells // half
    ins = [
        pltpu.make_async_copy(above_hbm, rim_ref.at[:, pl.ds(0, n_cols)], sems.at[0]),
        pltpu.make_async_copy(cot_hbm, rim_ref.at[:, pl.ds(n_cols, cells)], sems.at[1]),
        pltpu.make_async_copy(below_hbm, rim_ref.at[:, pl.ds(n_cols + cells, n_cols)], sems.at[2]),
    ]
    filters = pltpu.make_async_copy(mix_hbm, mix_ref, sems.at[3])
    outs = [
        pltpu.make_async_copy(
            turned_hbm.at[k],
            out_hbm.at[k, pl.ds(pair_out, turned_hbm.shape[1])],
            sems.at[4 + k],
        )
        for k in range(n_chan)
    ]
    for copy in ins + [filters] + outs:
        copy.start()
    for copy in ins:
        copy.wait()
    rim = rim_ref[...]
    wide = rim.astype(F32)
    taps = [moved(wide, -1, n_cols).astype(BF16), rim, moved(wide, 1, n_cols).astype(BF16)]
    for i in range(3):
        for j in range(3):
            first = (3 * i + j) * own_out
            start = (2 - i) * n_cols
            cols_ref[first : first + own_out, :] = taps[j][:, start : start + cells]
    filters.wait()
    for y in range(n_chan // n_half):
        part = lax.dot_general(
            mix_ref[:, y * pair_out : (y + 1) * pair_out],
            cols_ref[...],
            (((0,), (0,)), ((), ())),
            preferred_element_type=F32,
        ).astype(BF16)
        for h in range(n_half):
            k = y * n_half + h
            part_ref[k] = part[:, h * half : (h + 1) * half]
            copy = pltpu.make_async_copy(
                part_ref.at[k], out_hbm.at[k, pl.ds(0, pair_out)], sems.at[4 + n_chan + k]
            )
            copy.start()
            outs.append(copy)
    for copy in outs:
        copy.wait()


VM = pl.BlockSpec(memory_space=pltpu.VMEM)
FAR = pl.BlockSpec(memory_space=pl.ANY)
HBM = pl.BlockSpec(memory_space=pltpu.HBM)
SM = pl.BlockSpec(memory_space=pltpu.SMEM)


def run(kernel, in_specs, out_specs, outs, scratch, flops, *args):
    size = sum(a.size * a.dtype.itemsize for a in args + tuple(outs))
    return pl.pallas_call(
        kernel,
        out_shape=tuple(outs),
        in_specs=in_specs,
        out_specs=tuple(out_specs),
        scratch_shapes=scratch,
        cost_estimate=pl.CostEstimate(flops=flops, bytes_accessed=size, transcendentals=0),
        compiler_params=pltpu.CompilerParams(vmem_limit_bytes=16 << 20),
    )(*args)


def grad_hidden_parts(above, cot, below, mix, turned):
    n_chan, spare, half = turned.shape
    own_out, cells = cot.shape
    n_cols = above.shape[1]
    pair_out = mix.shape[1] * cells // (n_chan * half)
    return run(
        grad_hidden_kernel,
        [FAR, FAR, FAR, HBM, HBM],
        [VM, HBM],
        (
            shape((9 * own_out, cells), BF16),
            shape((n_chan, pair_out + spare, half), BF16),
        ),
        [
            pltpu.VMEM((own_out, cells + 2 * n_cols), BF16),
            pltpu.VMEM(mix.shape, BF16),
            pltpu.VMEM((n_chan, pair_out, half), BF16),
            pltpu.SemaphoreType.DMA((2 * n_chan + 4,)),
        ],
        2 * mix.size * cells,
        above,
        cot,
        below,
        mix,
        turned,
    )


def spread_kernel(hidden_ref, halo_ref, out_ref):
    n_chan, all_rows, half = out_ref.shape
    pair_out, n_cols = halo_ref.shape
    spare = all_rows - pair_out
    halo = jnp.concatenate(
        [halo_ref[q * spare : (q + 1) * spare, :] for q in range(half // n_cols)], axis=1
    )
    for k in range(n_chan):
        out_ref[k, :pair_out, :] = hidden_ref[...]
        out_ref[k, pair_out:, :] = halo


def grad_pre_kernel(side_ref, got_ref, slope_ref, patches_ref, pre_ref, keep_ref, give_ref):
    n_chan = got_ref.shape[0]
    pair_out = slope_ref.shape[0]
    own_out = pair_out // 2
    taps = patches_ref.shape[0] // n_chan
    total = got_ref[0, :pair_out, :].astype(F32)
    for k in range(1, n_chan):
        total += got_ref[k, :pair_out, :].astype(F32)
    pre = (total * slope_ref[...]).astype(BF16)
    pre_ref[...] = pre
    first = side_ref[0] == 0
    rows = taps // 2
    for k in range(n_chan):
        down = lax.dot_general(
            patches_ref[k * taps : (k + 1) * taps, :],
            pre,
            (((1,), (1,)), ((), ())),
            preferred_element_type=F32,
        )
        sides = [
            jnp.concatenate(
                [down[:rows, h * own_out : (h + 1) * own_out],
                 down[rows:, h * own_out : (h + 1) * own_out]],
                axis=1,
            )
            for h in range(2)
        ]
        keep_ref[k * rows : (k + 1) * rows, :] = jnp.where(first, sides[0], sides[1])
        give_ref[k * rows : (k + 1) * rows, :] = jnp.where(first, sides[1], sides[0]).astype(BF16)


def spread_parts(hidden, halo, n_chan):
    rows = hidden.shape[0] + halo.size // hidden.shape[1]
    (out,) = run(
        spread_kernel,
        [VM, VM],
        [VM],
        (shape((n_chan, rows, hidden.shape[1]), BF16),),
        [],
        0,
        hidden,
        halo,
    )
    return out


def grad_pre_parts(side, got, slope, patches):
    pair_out = slope.shape[0]
    down = (patches.shape[0] // 2, pair_out)
    return run(
        grad_pre_kernel,
        [SM, VM, VM, VM],
        [VM, VM, VM],
        (shape(slope.shape, BF16), shape(down, F32), shape(down, BF16)),
        [],
        2 * patches.size * pair_out,
        side,
        got,
        slope,
        patches,
    )


def grad_mix_kernel(
    core_ref, both_hbm, cols_ref, down_hbm, more_hbm, keep_ref, give_hbm, hidden_ref, down_ref,
    more_ref, give_ref, sems,
):
    n_group, rows, width = keep_ref.shape
    n_chan, _, half = both_hbm.shape
    all_out, cells = hidden_ref.shape
    taps = cols_ref.shape[0]
    n_half = cells // half
    pair_out = all_out * n_half // n_chan
    maps = []
    for k in range(n_chan):
        y, h = divmod(k, n_half)
        maps.append(
            pltpu.make_async_copy(
                both_hbm.at[k, pl.ds(0, pair_out)],
                hidden_ref.at[pl.ds(y * pair_out, pair_out), pl.ds(h * half, half)],
                sems.at[k],
            )
        )
    downs = [
        pltpu.make_async_copy(down_hbm, down_ref, sems.at[n_chan]),
        pltpu.make_async_copy(more_hbm, more_ref, sems.at[n_chan + 1]),
    ]
    for copy in maps + downs:
        copy.start()
    first = core_ref[0] == 0
    for copy in downs:
        copy.wait()
    parts = 2
    size = all_out // parts
    step = n_group // parts
    blank = jnp.zeros((size, width - taps - down_ref.shape[1]), F32)
    for part in range(parts):
        for copy in maps[part * n_chan // parts : (part + 1) * n_chan // parts]:
            copy.wait()
        at = slice(part * size, (part + 1) * size)
        total = lax.dot_general(
            hidden_ref[at, :],
            cols_ref[...],
            (((1,), (1,)), ((), ())),
            preferred_element_type=F32,
        )
        extra = down_ref[at, :] + more_ref[at, :].astype(F32)
        total = jnp.concatenate([total, extra, blank], axis=1)
        total = total.reshape(step, 2, rows, width)
        to = slice(part * step, (part + 1) * step)
        keep_ref[to] = jnp.where(first, total[:, 0], total[:, 1])
        give_ref[to] = jnp.where(first, total[:, 1], total[:, 0]).astype(BF16)
    give = pltpu.make_async_copy(give_ref, give_hbm, sems.at[n_chan + 2])
    give.start()
    give.wait()


def grad_mix_parts(core, both, cols, down, more, n_tile, width):
    n_chan, _, half = both.shape
    all_out = down.shape[0]
    rows = all_out // n_tile
    return run(
        grad_mix_kernel,
        [SM, HBM, VM, FAR, FAR],
        [VM, FAR],
        (shape((n_tile // 2, rows, width), F32), shape((n_tile // 2, rows, width), BF16)),
        [
            pltpu.VMEM((all_out, cols.shape[1]), BF16),
            pltpu.VMEM(down.shape, F32),
            pltpu.VMEM(down.shape, BF16),
            pltpu.VMEM((n_tile // 2, rows, width), BF16),
            pltpu.SemaphoreType.DMA((n_chan + 3,)),
        ],
        2 * all_out * cols.size,
        core,
        both,
        cols,
        down,
        more,
    )


def mixed_kernel(mix_ref, both_ref, out_ref):
    own_out, cells = out_ref.shape
    n_chan, all_rows, half = both_ref.shape
    n_half = cells // half
    n_y = n_chan // n_half
    pair_out = mix_ref.shape[1] // n_y
    spare = all_rows - pair_out
    n_cols = spare * half // pair_out

    def edge(k):
        return jnp.concatenate(
            [both_ref[k, pair_out:, q * n_cols : (q + 1) * n_cols] for q in range(half // n_cols)]
        )

    hidden = jnp.concatenate(
        [
            jnp.concatenate(
                [edge(y * n_half + n_half - 1)]
                + [both_ref[y * n_half + h, :pair_out, :] for h in range(n_half)]
                + [edge(y * n_half)],
                axis=1,
            )
            for y in range(n_y)
        ]
    )
    total = jnp.zeros((3 * own_out, cells), F32)
    for i in range(3):
        total += jnp.dot(
            mix_ref[3 * own_out * i : 3 * own_out * (i + 1), :],
            hidden[:, i * n_cols : i * n_cols + cells],
            preferred_element_type=F32,
        )
    out_ref[...] = (
        moved(total[:own_out], 1, n_cols)
        + total[own_out : 2 * own_out]
        + moved(total[2 * own_out :], -1, n_cols)
    ).astype(BF16)


def per_device(image, w_down, w_mix, cotangent):
    n_y, n_xl = (lax.axis_size(a) for a in CHAN)
    n_z, n_xh, n_core = (lax.axis_size(a) for a in TILE)
    n_chan = n_y * n_xl
    n_tile = n_z * n_xh * n_core
    own_in, _, in_cols = image.shape
    own_out, n_rows, n_cols = cotangent.shape
    cells = n_rows * n_cols
    half = cells // n_xl
    pair_out = n_xl * own_out
    all_in = n_chan * own_in
    all_out = n_chan * own_out
    taps = 4 * own_in
    groups = n_tile // n_chan
    group = own_in // groups
    scale = 1.0 / math.sqrt(cells * n_tile)
    ahead = [(i, i + 1) for i in range(n_tile - 1)]
    back = [(i + 1, i) for i in range(n_tile - 1)]
    flip = [(0, 1), (1, 0)]
    side = lax.axis_index("xl")
    first = side == 0

    above = lax.ppermute(cotangent[:, n_rows - 1], TILE, ahead)
    below = lax.ppermute(cotangent[:, 0], TILE, back)

    even_odd = (
        jnp.arange(in_cols)[:, None, None]
        == 2 * jnp.arange(n_cols)[None, None, :] + jnp.arange(2)[None, :, None]
    ).astype(BF16)
    sent = dot("crax,xbw->rabcw", image.reshape(own_in, n_rows, 2, in_cols), even_odd)
    sent = sent.astype(BF16).reshape(n_xl, n_rows // n_xl, 2, 2, groups, group, n_cols)
    sent = jnp.transpose(sent, (0, 2, 4, 3, 5, 1, 6)).reshape(n_xl, taps, half)
    sent = jnp.broadcast_to(sent[None], (n_y,) + sent.shape).reshape(n_chan, taps, half)
    patches = swap(sent, CHAN)

    mix = jnp.transpose(w_mix, (0, 1, 3, 2)).reshape(9 * own_out, all_out)
    turned = jnp.transpose(w_down.reshape(2, 2, n_y, n_xl, own_in, own_out), (2, 5, 3, 0, 1, 4))
    wide = n_xl * taps
    spare = own_out * wide // half
    turned = turned.reshape(n_y, own_out // spare, spare, wide)
    turned = jnp.transpose(turned, (0, 2, 1, 3)).reshape(n_y, 1, spare, half)
    turned = jnp.broadcast_to(turned, (n_y, n_xl, spare, half)).reshape(n_chan, spare, half)
    other_down = lax.ppermute(w_down, "xl", flip)
    cols, partial = grad_hidden_parts(
        above,
        cotangent.reshape(own_out, cells),
        below,
        mix,
        turned,
    )
    patches, partial, other_down = lax.optimization_barrier((patches, partial, other_down))
    partial = swap(partial, CHAN)

    down = jnp.stack([jnp.where(first, w_down, other_down), jnp.where(first, other_down, w_down)])
    down = down.reshape(n_xl, 2, 2, n_chan, groups, group, own_out)
    down = jnp.transpose(down, (0, 6, 3, 1, 4, 2, 5)).reshape(pair_out, 4 * all_in)
    patches = patches.reshape(4 * all_in, half)
    preact = dot("dk,kq->dq", down, patches)
    cdf = normal_cdf(preact)
    slope = cdf + preact * normal_pdf(preact)
    hidden = (preact * cdf).astype(BF16)
    halo = jnp.where(first, hidden[:, :n_cols], hidden[:, half - n_cols :])
    halo = lax.ppermute(halo, ("xl",) + TILE, back + [(n_tile + i, n_tile + j) for i, j in ahead])
    both = spread_parts(hidden, halo, n_chan)
    both, slope, partial = lax.optimization_barrier((both, slope, partial))
    both = swap(both, CHAN)
    grad_pre, down_keep, down_give = grad_pre_parts(side.reshape(1), partial, slope, patches)
    down_more = lax.ppermute(down_give, "xl", flip)
    all_pre = jnp.broadcast_to(grad_pre[None], (n_y,) + grad_pre.shape)
    both, down_more, all_pre = lax.optimization_barrier((both, down_more, all_pre))
    all_pre = swap(all_pre, "y")

    rows = all_out // n_tile
    width = 12 * own_out
    core = lax.axis_index("core").reshape(1)
    keep, give = grad_mix_parts(core, both, cols, down_keep, down_more, n_tile, width)
    total = keep + lax.ppermute(give, "core", flip).astype(F32)
    total, all_pre = lax.optimization_barrier((total.astype(BF16), all_pre))
    total = swap(total, ("z", "xh"))
    total = jnp.sum(total.astype(F32), axis=0) * scale
    grad_mix = total[:, : 9 * own_out].reshape(rows, 3, 3, own_out)
    piece = total[:, 9 * own_out : 11 * own_out].reshape(2, group, 2, own_out)
    grad_down = jnp.transpose(piece, (1, 2, 0, 3))

    (mixed,) = call(
        mixed_kernel, (shape((own_out, cells), BF16),), 2 * mix.size * cells, mix, both
    )
    mixed = mixed.reshape(own_out, n_rows, n_cols)

    turned = partial[:, pair_out:].reshape(n_chan, spare, own_out // spare, wide)
    turned = jnp.transpose(turned, (0, 2, 1, 3)).reshape(n_y, pair_out, wide)
    grad_image = dot("ydk,ydq->kq", turned, all_pre)
    grad_image = grad_image.astype(BF16).reshape(n_xl, taps, half)
    mine = jnp.where(first, grad_image[0], grad_image[1])
    theirs = lax.ppermute(jnp.where(first, grad_image[1], grad_image[0]), "xl", flip)
    grad_image = jnp.concatenate(
        [jnp.where(first, mine, theirs), jnp.where(first, theirs, mine)], axis=1
    )
    grad_image = grad_image.reshape(2, 2, own_in, n_rows, n_cols)
    grad_image = dot("abcrw,xbw->crax", grad_image, even_odd)
    grad_image = grad_image.astype(BF16).reshape(image.shape)
    return (mixed, grad_mix, grad_down, grad_image)


def solution(mesh):
    grid = mesh.devices
    n_chan, n_tile = grid.shape
    split = Mesh(grid.reshape(n_chan // 2, 2, n_tile // 4, 2, 2), CHAN + TILE)
    return jax.shard_map(
        per_device,
        mesh=split,
        in_specs=(
            P(CHAN, TILE, None),
            P(None, None, None, CHAN),
            P(None, None, None, CHAN),
            P(CHAN, TILE, None),
        ),
        out_specs=(
            P(CHAN, TILE, None),
            P(TILE, None, None, CHAN),
            P(TILE, None, None, CHAN),
            P(CHAN, TILE, None),
        ),
        check_vma=False,
    )
```

```python
import math

import jax
import jax.numpy as jnp
from jax import lax
from jax.experimental import pallas as pl
from jax.experimental.pallas import tpu as pltpu
from jax.sharding import Mesh, PartitionSpec as P

CHAN = ("y", "xl")
TILE = ("z", "xh", "core")
BF16 = jnp.bfloat16
F32 = jnp.float32


def normal_cdf(value):
    return 0.5 * (1.0 + jax.scipy.special.erf(value / math.sqrt(2.0)))


def normal_pdf(value):
    return jnp.exp(-0.5 * value * value) / math.sqrt(2.0 * math.pi)


def dot(spec, left, right):
    return jnp.einsum(spec, left, right, preferred_element_type=F32)


def swap(block, axis):
    return lax.all_to_all(block, axis, 0, 0)


def halved(block, axis, dim):
    mine = lax.axis_index(axis)
    keep = lax.dynamic_index_in_dim(block, mine, dim, keepdims=False)
    give = lax.dynamic_index_in_dim(block, 1 - mine, dim, keepdims=False).astype(BF16)
    return keep + lax.ppermute(give, axis, [(0, 1), (1, 0)]).astype(F32)


def call(kernel, outs, flops, *args):
    whole = pl.BlockSpec(memory_space=pltpu.VMEM)
    moved = sum(a.size * a.dtype.itemsize for a in args + tuple(outs))
    return pl.pallas_call(
        kernel,
        out_shape=tuple(outs),
        in_specs=[whole] * len(args),
        out_specs=(whole,) * len(outs),
        cost_estimate=pl.CostEstimate(flops=flops, bytes_accessed=moved, transcendentals=0),
        compiler_params=pltpu.CompilerParams(vmem_limit_bytes=12 << 20),
    )(*args)


def call_core(kernel, outs, flops, core, *args):
    whole = pl.BlockSpec(memory_space=pltpu.VMEM)
    moved = sum(a.size * a.dtype.itemsize for a in args + tuple(outs))
    return pl.pallas_call(
        kernel,
        out_shape=tuple(outs),
        in_specs=[pl.BlockSpec(memory_space=pltpu.SMEM)] + [whole] * len(args),
        out_specs=(whole,) * len(outs),
        cost_estimate=pl.CostEstimate(flops=flops, bytes_accessed=moved, transcendentals=0),
        compiler_params=pltpu.CompilerParams(vmem_limit_bytes=12 << 20),
    )(core, *args)


def shape(dims, dtype):
    return jax.ShapeDtypeStruct(dims, dtype)


def moved(block, step, n_cols):
    width = block.shape[1]
    column = lax.rem(lax.broadcasted_iota(jnp.int32, block.shape, 1), n_cols)
    if step > 0:
        return jnp.where(column > 0, pltpu.roll(block, 1, 1), 0.0)
    return jnp.where(column < n_cols - 1, pltpu.roll(block, width - 1, 1), 0.0)


def grad_hidden_kernel(above_ref, cot_ref, below_ref, mix_ref, turned_ref, cols_ref, out_ref):
    own_out, n_cols = above_ref.shape
    cells = cot_ref.shape[1]
    n_chan, spare, half = turned_ref.shape
    pair_out = out_ref.shape[1] - spare
    n_half = cells // half
    rim = jnp.concatenate([above_ref[...], cot_ref[...], below_ref[...]], axis=1)
    wide = rim.astype(F32)
    taps = [moved(wide, -1, n_cols).astype(BF16), rim, moved(wide, 1, n_cols).astype(BF16)]
    for i in range(3):
        for j in range(3):
            first = (3 * i + j) * own_out
            start = (2 - i) * n_cols
            cols_ref[first : first + own_out, :] = taps[j][:, start : start + cells]
    for y in range(n_chan // n_half):
        part = lax.dot_general(
            mix_ref[:, y * pair_out : (y + 1) * pair_out],
            cols_ref[...],
            (((0,), (0,)), ((), ())),
            preferred_element_type=F32,
        ).astype(BF16)
        for h in range(n_half):
            out_ref[y * n_half + h, :pair_out, :] = part[:, h * half : (h + 1) * half]
            out_ref[y * n_half + h, pair_out:, :] = turned_ref[y * n_half + h]


def spread_kernel(hidden_ref, halo_ref, out_ref):
    n_chan, all_rows, half = out_ref.shape
    pair_out, n_cols = halo_ref.shape
    spare = all_rows - pair_out
    halo = jnp.concatenate(
        [halo_ref[q * spare : (q + 1) * spare, :] for q in range(half // n_cols)], axis=1
    )
    for k in range(n_chan):
        out_ref[k, :pair_out, :] = hidden_ref[...]
        out_ref[k, pair_out:, :] = halo


def grad_pre_kernel(side_ref, got_ref, slope_ref, patches_ref, pre_ref, keep_ref, give_ref):
    n_chan = got_ref.shape[0]
    pair_out = slope_ref.shape[0]
    own_out = pair_out // 2
    taps = patches_ref.shape[0] // n_chan
    total = got_ref[0, :pair_out, :].astype(F32)
    for k in range(1, n_chan):
        total += got_ref[k, :pair_out, :].astype(F32)
    pre = (total * slope_ref[...]).astype(BF16)
    pre_ref[...] = pre
    first = side_ref[0] == 0
    rows = taps // 2
    for k in range(n_chan):
        down = lax.dot_general(
            patches_ref[k * taps : (k + 1) * taps, :],
            pre,
            (((1,), (1,)), ((), ())),
            preferred_element_type=F32,
        )
        sides = [
            jnp.concatenate(
                [down[:rows, h * own_out : (h + 1) * own_out],
                 down[rows:, h * own_out : (h + 1) * own_out]],
                axis=1,
            )
            for h in range(2)
        ]
        keep_ref[k * rows : (k + 1) * rows, :] = jnp.where(first, sides[0], sides[1])
        give_ref[k * rows : (k + 1) * rows, :] = jnp.where(first, sides[1], sides[0]).astype(BF16)


def grad_mix_kernel(core_ref, both_ref, cols_ref, down_ref, more_ref, keep_ref, give_ref):
    n_group, rows, width = keep_ref.shape
    n_chan, _, half = both_ref.shape
    taps, cells = cols_ref.shape
    n_half = cells // half
    pair_out = n_group * 2 * rows * n_half // n_chan
    first = core_ref[0] == 0
    step = pair_out // (2 * rows)
    blank = jnp.zeros((pair_out, width - taps - down_ref.shape[1]), F32)
    for y in range(n_chan // n_half):
        hidden = jnp.concatenate(
            [both_ref[y * n_half + h, :pair_out, :] for h in range(n_half)], axis=1
        )
        total = lax.dot_general(
            hidden, cols_ref[...], (((1,), (1,)), ((), ())), preferred_element_type=F32
        )
        at = slice(y * pair_out, (y + 1) * pair_out)
        extra = down_ref[at, :] + more_ref[at, :].astype(F32)
        total = jnp.concatenate([total, extra, blank], axis=1)
        total = total.reshape(step, 2, rows, width)
        keep_ref[y * step : (y + 1) * step] = jnp.where(first, total[:, 0], total[:, 1])
        give_ref[y * step : (y + 1) * step] = jnp.where(first, total[:, 1], total[:, 0]).astype(
            BF16
        )


def mixed_kernel(mix_ref, both_ref, out_ref):
    own_out, cells = out_ref.shape
    n_chan, all_rows, half = both_ref.shape
    n_half = cells // half
    n_y = n_chan // n_half
    pair_out = mix_ref.shape[1] // n_y
    spare = all_rows - pair_out
    n_cols = spare * half // pair_out

    def edge(k):
        return jnp.concatenate(
            [both_ref[k, pair_out:, q * n_cols : (q + 1) * n_cols] for q in range(half // n_cols)]
        )

    hidden = jnp.concatenate(
        [
            jnp.concatenate(
                [edge(y * n_half + n_half - 1)]
                + [both_ref[y * n_half + h, :pair_out, :] for h in range(n_half)]
                + [edge(y * n_half)],
                axis=1,
            )
            for y in range(n_y)
        ]
    )
    total = jnp.zeros((3 * own_out, cells), F32)
    for i in range(3):
        total += jnp.dot(
            mix_ref[3 * own_out * i : 3 * own_out * (i + 1), :],
            hidden[:, i * n_cols : i * n_cols + cells],
            preferred_element_type=F32,
        )
    out_ref[...] = (
        moved(total[:own_out], 1, n_cols)
        + total[own_out : 2 * own_out]
        + moved(total[2 * own_out :], -1, n_cols)
    ).astype(BF16)


def per_device(image, w_down, w_mix, cotangent):
    n_y, n_xl = (lax.axis_size(a) for a in CHAN)
    n_z, n_xh, n_core = (lax.axis_size(a) for a in TILE)
    n_chan = n_y * n_xl
    n_tile = n_z * n_xh * n_core
    own_in, _, in_cols = image.shape
    own_out, n_rows, n_cols = cotangent.shape
    cells = n_rows * n_cols
    half = cells // n_xl
    pair_out = n_xl * own_out
    all_in = n_chan * own_in
    all_out = n_chan * own_out
    taps = 4 * own_in
    groups = n_tile // n_chan
    group = own_in // groups
    scale = 1.0 / math.sqrt(cells * n_tile)
    ahead = [(i, i + 1) for i in range(n_tile - 1)]
    back = [(i + 1, i) for i in range(n_tile - 1)]
    flip = [(0, 1), (1, 0)]
    side = lax.axis_index("xl")
    first = side == 0

    other_down = lax.ppermute(w_down, "xl", flip)

    even_odd = (
        jnp.arange(in_cols)[:, None, None]
        == 2 * jnp.arange(n_cols)[None, None, :] + jnp.arange(2)[None, :, None]
    ).astype(BF16)
    sent = dot("crax,xbw->rabcw", image.reshape(own_in, n_rows, 2, in_cols), even_odd)
    sent = sent.astype(BF16).reshape(n_xl, n_rows // n_xl, 2, 2, groups, group, n_cols)
    sent = jnp.transpose(sent, (0, 2, 4, 3, 5, 1, 6)).reshape(n_xl, taps, half)
    sent = jnp.broadcast_to(sent[None], (n_y,) + sent.shape).reshape(n_chan, taps, half)
    sent, cotangent = lax.optimization_barrier((sent, cotangent))
    patches = swap(sent, CHAN)

    above = lax.ppermute(cotangent[:, n_rows - 1], TILE, ahead)
    below = lax.ppermute(cotangent[:, 0], TILE, back)

    mix = jnp.transpose(w_mix, (0, 1, 3, 2)).reshape(9 * own_out, all_out)
    turned = jnp.transpose(w_down.reshape(2, 2, n_y, n_xl, own_in, own_out), (2, 5, 3, 0, 1, 4))
    wide = n_xl * taps
    spare = own_out * wide // half
    turned = turned.reshape(n_y, own_out // spare, spare, wide)
    turned = jnp.transpose(turned, (0, 2, 1, 3)).reshape(n_y, 1, spare, half)
    turned = jnp.broadcast_to(turned, (n_y, n_xl, spare, half)).reshape(n_chan, spare, half)
    cols, partial = call(
        grad_hidden_kernel,
        (
            shape((9 * own_out, cells), BF16),
            shape((n_chan, pair_out + spare, half), BF16),
        ),
        2 * mix.size * cells,
        above,
        cotangent.reshape(own_out, cells),
        below,
        mix,
        turned,
    )
    patches, partial, other_down = lax.optimization_barrier((patches, partial, other_down))
    partial = swap(partial, CHAN)

    down = jnp.stack([jnp.where(first, w_down, other_down), jnp.where(first, other_down, w_down)])
    down = down.reshape(n_xl, 2, 2, n_chan, groups, group, own_out)
    down = jnp.transpose(down, (0, 6, 3, 1, 4, 2, 5)).reshape(pair_out, 4 * all_in)
    patches = patches.reshape(4 * all_in, half)
    preact = dot("dk,kq->dq", down, patches)
    cdf = normal_cdf(preact)
    slope = cdf + preact * normal_pdf(preact)
    hidden = (preact * cdf).astype(BF16)
    halo = jnp.where(first, hidden[:, :n_cols], hidden[:, half - n_cols :])
    halo = lax.ppermute(halo, ("xl",) + TILE, back + [(n_tile + i, n_tile + j) for i, j in ahead])
    (both,) = call(
        spread_kernel,
        (shape((n_chan, pair_out + pair_out * n_cols // half, half), BF16),),
        0,
        hidden,
        halo,
    )
    both, slope, partial = lax.optimization_barrier((both, slope, partial))
    both = swap(both, CHAN)
    grad_pre, down_keep, down_give = call_core(
        grad_pre_kernel,
        (
            shape((pair_out, half), BF16),
            shape((all_out, 2 * own_out), F32),
            shape((all_out, 2 * own_out), BF16),
        ),
        2 * patches.size * pair_out,
        side.reshape(1),
        partial,
        slope,
        patches,
    )
    down_more = lax.ppermute(down_give, "xl", flip)
    near = [grad_pre] + [
        lax.ppermute(grad_pre, "y", [(i, (i + k) % n_y) for i in range(n_y)])
        for k in range(1, n_y)
    ]

    rows = all_out // n_tile
    width = 12 * own_out
    keep, give = call_core(
        grad_mix_kernel,
        (
            shape((n_z * n_xh, rows, width), F32),
            shape((n_z * n_xh, rows, width), BF16),
        ),
        2 * mix.size * cells,
        lax.axis_index("core").reshape(1),
        both,
        cols,
        down_keep,
        down_more,
    )
    total = keep + lax.ppermute(give, "core", flip).astype(F32)
    total = swap(total.astype(BF16), ("z", "xh"))
    total = jnp.sum(total.astype(F32), axis=0) * scale
    grad_mix = total[:, : 9 * own_out].reshape(rows, 3, 3, own_out)
    piece = total[:, 9 * own_out : 11 * own_out].reshape(2, group, 2, own_out)
    grad_down = jnp.transpose(piece, (1, 2, 0, 3))

    (mixed,) = call(
        mixed_kernel, (shape((own_out, cells), BF16),), 2 * mix.size * cells, mix, both
    )
    mixed = mixed.reshape(own_out, n_rows, n_cols)

    turned = partial[:, pair_out:].reshape(n_chan, spare, own_out // spare, wide)
    turned = jnp.transpose(turned, (0, 2, 1, 3)).reshape(n_y, pair_out, wide)
    line = lax.axis_index("y")
    grad_image = sum(
        dot("dk,dq->kq", lax.dynamic_index_in_dim(turned, (line - k) % n_y, 0, False), near[k])
        for k in range(n_y)
    )
    grad_image = grad_image.astype(BF16).reshape(n_xl, taps, half)
    mine = jnp.where(first, grad_image[0], grad_image[1])
    theirs = lax.ppermute(jnp.where(first, grad_image[1], grad_image[0]), "xl", flip)
    grad_image = jnp.concatenate(
        [jnp.where(first, mine, theirs), jnp.where(first, theirs, mine)], axis=1
    )
    grad_image = grad_image.reshape(2, 2, own_in, n_rows, n_cols)
    grad_image = dot("abcrw,xbw->crax", grad_image, even_odd)
    grad_image = grad_image.astype(BF16).reshape(image.shape)
    return (mixed, grad_mix, grad_down, grad_image)


def solution(mesh):
    grid = mesh.devices
    n_chan, n_tile = grid.shape
    split = Mesh(grid.reshape(n_chan // 2, 2, n_tile // 4, 2, 2), CHAN + TILE)
    return jax.shard_map(
        per_device,
        mesh=split,
        in_specs=(
            P(CHAN, TILE, None),
            P(None, None, None, CHAN),
            P(None, None, None, CHAN),
            P(CHAN, TILE, None),
        ),
        out_specs=(
            P(CHAN, TILE, None),
            P(TILE, None, None, CHAN),
            P(TILE, None, None, CHAN),
            P(CHAN, TILE, None),
        ),
        check_vma=False,
    )
```

```python
import math

import jax
import jax.numpy as jnp
from jax import lax
from jax.experimental import pallas as pl
from jax.experimental.pallas import tpu as pltpu
from jax.sharding import Mesh, PartitionSpec as P

CHAN = ("y", "xl")
TILE = ("z", "xh", "core")
BF16 = jnp.bfloat16
F32 = jnp.float32


def normal_cdf(value):
    return 0.5 * (1.0 + jax.scipy.special.erf(value / math.sqrt(2.0)))


def normal_pdf(value):
    return jnp.exp(-0.5 * value * value) / math.sqrt(2.0 * math.pi)


def dot(spec, left, right):
    return jnp.einsum(spec, left, right, preferred_element_type=F32)


def swap(block, axis):
    return lax.all_to_all(block, axis, 0, 0)


def halved(block, axis, dim):
    mine = lax.axis_index(axis)
    keep = lax.dynamic_index_in_dim(block, mine, dim, keepdims=False)
    give = lax.dynamic_index_in_dim(block, 1 - mine, dim, keepdims=False).astype(BF16)
    return keep + lax.ppermute(give, axis, [(0, 1), (1, 0)]).astype(F32)


def call(kernel, outs, flops, *args):
    whole = pl.BlockSpec(memory_space=pltpu.VMEM)
    moved = sum(a.size * a.dtype.itemsize for a in args + tuple(outs))
    return pl.pallas_call(
        kernel,
        out_shape=tuple(outs),
        in_specs=[whole] * len(args),
        out_specs=(whole,) * len(outs),
        cost_estimate=pl.CostEstimate(flops=flops, bytes_accessed=moved, transcendentals=0),
        compiler_params=pltpu.CompilerParams(vmem_limit_bytes=12 << 20),
    )(*args)


def call_core(kernel, outs, flops, core, *args):
    whole = pl.BlockSpec(memory_space=pltpu.VMEM)
    moved = sum(a.size * a.dtype.itemsize for a in args + tuple(outs))
    return pl.pallas_call(
        kernel,
        out_shape=tuple(outs),
        in_specs=[pl.BlockSpec(memory_space=pltpu.SMEM)] + [whole] * len(args),
        out_specs=(whole,) * len(outs),
        cost_estimate=pl.CostEstimate(flops=flops, bytes_accessed=moved, transcendentals=0),
        compiler_params=pltpu.CompilerParams(vmem_limit_bytes=12 << 20),
    )(core, *args)


def shape(dims, dtype):
    return jax.ShapeDtypeStruct(dims, dtype)


def moved(block, step, n_cols):
    width = block.shape[1]
    column = lax.rem(lax.broadcasted_iota(jnp.int32, block.shape, 1), n_cols)
    if step > 0:
        return jnp.where(column > 0, pltpu.roll(block, 1, 1), 0.0)
    return jnp.where(column < n_cols - 1, pltpu.roll(block, width - 1, 1), 0.0)


def grad_hidden_kernel(above_ref, cot_ref, below_ref, mix_ref, turned_ref, cols_ref, out_ref):
    own_out, n_cols = above_ref.shape
    cells = cot_ref.shape[1]
    n_chan, spare, half = turned_ref.shape
    pair_out = out_ref.shape[1] - spare
    n_half = cells // half
    rim = jnp.concatenate([above_ref[...], cot_ref[...], below_ref[...]], axis=1)
    wide = rim.astype(F32)
    taps = [moved(wide, -1, n_cols).astype(BF16), rim, moved(wide, 1, n_cols).astype(BF16)]
    for i in range(3):
        for j in range(3):
            first = (3 * i + j) * own_out
            start = (2 - i) * n_cols
            cols_ref[first : first + own_out, :] = taps[j][:, start : start + cells]
    for y in range(n_chan // n_half):
        part = lax.dot_general(
            mix_ref[:, y * pair_out : (y + 1) * pair_out],
            cols_ref[...],
            (((0,), (0,)), ((), ())),
            preferred_element_type=F32,
        ).astype(BF16)
        for h in range(n_half):
            out_ref[y * n_half + h, :pair_out, :] = part[:, h * half : (h + 1) * half]
            out_ref[y * n_half + h, pair_out:, :] = turned_ref[y * n_half + h]


def spread_kernel(hidden_ref, halo_ref, out_ref):
    n_chan, all_rows, half = out_ref.shape
    pair_out, n_cols = halo_ref.shape
    spare = all_rows - pair_out
    halo = jnp.concatenate(
        [halo_ref[q * spare : (q + 1) * spare, :] for q in range(half // n_cols)], axis=1
    )
    for k in range(n_chan):
        out_ref[k, :pair_out, :] = hidden_ref[...]
        out_ref[k, pair_out:, :] = halo


def grad_pre_kernel(side_ref, got_ref, slope_ref, patches_ref, pre_ref, keep_ref, give_ref):
    n_chan = got_ref.shape[0]
    pair_out = slope_ref.shape[0]
    own_out = pair_out // 2
    taps = patches_ref.shape[0] // n_chan
    total = got_ref[0, :pair_out, :].astype(F32)
    for k in range(1, n_chan):
        total += got_ref[k, :pair_out, :].astype(F32)
    pre = (total * slope_ref[...]).astype(BF16)
    pre_ref[...] = pre
    first = side_ref[0] == 0
    rows = taps // 2
    for k in range(n_chan):
        down = lax.dot_general(
            patches_ref[k * taps : (k + 1) * taps, :],
            pre,
            (((1,), (1,)), ((), ())),
            preferred_element_type=F32,
        )
        sides = [
            jnp.concatenate(
                [down[:rows, h * own_out : (h + 1) * own_out],
                 down[rows:, h * own_out : (h + 1) * own_out]],
                axis=1,
            )
            for h in range(2)
        ]
        keep_ref[k * rows : (k + 1) * rows, :] = jnp.where(first, sides[0], sides[1])
        give_ref[k * rows : (k + 1) * rows, :] = jnp.where(first, sides[1], sides[0]).astype(BF16)


VM = pl.BlockSpec(memory_space=pltpu.VMEM)
FAR = pl.BlockSpec(memory_space=pl.ANY)
HBM = pl.BlockSpec(memory_space=pltpu.HBM)
SM = pl.BlockSpec(memory_space=pltpu.SMEM)


def run(kernel, in_specs, out_specs, outs, scratch, flops, *args):
    size = sum(a.size * a.dtype.itemsize for a in args + tuple(outs))
    return pl.pallas_call(
        kernel,
        out_shape=tuple(outs),
        in_specs=in_specs,
        out_specs=tuple(out_specs),
        scratch_shapes=scratch,
        cost_estimate=pl.CostEstimate(flops=flops, bytes_accessed=size, transcendentals=0),
        compiler_params=pltpu.CompilerParams(vmem_limit_bytes=16 << 20),
    )(*args)


def grad_mix_kernel(
    core_ref, both_hbm, cols_ref, down_hbm, more_hbm, keep_ref, give_hbm, hidden_ref, down_ref,
    more_ref, give_ref, sems,
):
    n_group, rows, width = keep_ref.shape
    n_chan, _, half = both_hbm.shape
    all_out, cells = hidden_ref.shape
    taps = cols_ref.shape[0]
    n_half = cells // half
    pair_out = all_out * n_half // n_chan
    maps = []
    for k in range(n_chan):
        y, h = divmod(k, n_half)
        maps.append(
            pltpu.make_async_copy(
                both_hbm.at[k, pl.ds(0, pair_out)],
                hidden_ref.at[pl.ds(y * pair_out, pair_out), pl.ds(h * half, half)],
                sems.at[k],
            )
        )
    downs = [
        pltpu.make_async_copy(down_hbm, down_ref, sems.at[n_chan]),
        pltpu.make_async_copy(more_hbm, more_ref, sems.at[n_chan + 1]),
    ]
    for copy in maps + downs:
        copy.start()
    first = core_ref[0] == 0
    for copy in downs:
        copy.wait()
    parts = 2
    size = all_out // parts
    step = n_group // parts
    blank = jnp.zeros((size, width - taps - down_ref.shape[1]), F32)
    for part in range(parts):
        for copy in maps[part * n_chan // parts : (part + 1) * n_chan // parts]:
            copy.wait()
        at = slice(part * size, (part + 1) * size)
        total = lax.dot_general(
            hidden_ref[at, :],
            cols_ref[...],
            (((1,), (1,)), ((), ())),
            preferred_element_type=F32,
        )
        extra = down_ref[at, :] + more_ref[at, :].astype(F32)
        total = jnp.concatenate([total, extra, blank], axis=1)
        total = total.reshape(step, 2, rows, width)
        to = slice(part * step, (part + 1) * step)
        keep_ref[to] = jnp.where(first, total[:, 0], total[:, 1])
        give_ref[to] = jnp.where(first, total[:, 1], total[:, 0]).astype(BF16)
    give = pltpu.make_async_copy(give_ref, give_hbm, sems.at[n_chan + 2])
    give.start()
    give.wait()


def grad_mix_parts(core, both, cols, down, more, n_tile, width):
    n_chan, _, half = both.shape
    all_out = down.shape[0]
    rows = all_out // n_tile
    return run(
        grad_mix_kernel,
        [SM, HBM, VM, FAR, FAR],
        [VM, FAR],
        (shape((n_tile // 2, rows, width), F32), shape((n_tile // 2, rows, width), BF16)),
        [
            pltpu.VMEM((all_out, cols.shape[1]), BF16),
            pltpu.VMEM(down.shape, F32),
            pltpu.VMEM(down.shape, BF16),
            pltpu.VMEM((n_tile // 2, rows, width), BF16),
            pltpu.SemaphoreType.DMA((n_chan + 3,)),
        ],
        2 * all_out * cols.size,
        core,
        both,
        cols,
        down,
        more,
    )


def mixed_kernel(mix_ref, both_ref, out_ref):
    own_out, cells = out_ref.shape
    n_chan, all_rows, half = both_ref.shape
    n_half = cells // half
    n_y = n_chan // n_half
    pair_out = mix_ref.shape[1] // n_y
    spare = all_rows - pair_out
    n_cols = spare * half // pair_out

    def edge(k):
        return jnp.concatenate(
            [both_ref[k, pair_out:, q * n_cols : (q + 1) * n_cols] for q in range(half // n_cols)]
        )

    hidden = jnp.concatenate(
        [
            jnp.concatenate(
                [edge(y * n_half + n_half - 1)]
                + [both_ref[y * n_half + h, :pair_out, :] for h in range(n_half)]
                + [edge(y * n_half)],
                axis=1,
            )
            for y in range(n_y)
        ]
    )
    total = jnp.zeros((3 * own_out, cells), F32)
    for i in range(3):
        total += jnp.dot(
            mix_ref[3 * own_out * i : 3 * own_out * (i + 1), :],
            hidden[:, i * n_cols : i * n_cols + cells],
            preferred_element_type=F32,
        )
    out_ref[...] = (
        moved(total[:own_out], 1, n_cols)
        + total[own_out : 2 * own_out]
        + moved(total[2 * own_out :], -1, n_cols)
    ).astype(BF16)


def per_device(image, w_down, w_mix, cotangent):
    n_y, n_xl = (lax.axis_size(a) for a in CHAN)
    n_z, n_xh, n_core = (lax.axis_size(a) for a in TILE)
    n_chan = n_y * n_xl
    n_tile = n_z * n_xh * n_core
    own_in, _, in_cols = image.shape
    own_out, n_rows, n_cols = cotangent.shape
    cells = n_rows * n_cols
    half = cells // n_xl
    pair_out = n_xl * own_out
    all_in = n_chan * own_in
    all_out = n_chan * own_out
    taps = 4 * own_in
    groups = n_tile // n_chan
    group = own_in // groups
    scale = 1.0 / math.sqrt(cells * n_tile)
    ahead = [(i, i + 1) for i in range(n_tile - 1)]
    back = [(i + 1, i) for i in range(n_tile - 1)]
    flip = [(0, 1), (1, 0)]
    side = lax.axis_index("xl")
    first = side == 0

    other_down = lax.ppermute(w_down, "xl", flip)

    even_odd = (
        jnp.arange(in_cols)[:, None, None]
        == 2 * jnp.arange(n_cols)[None, None, :] + jnp.arange(2)[None, :, None]
    ).astype(BF16)
    sent = dot("crax,xbw->rabcw", image.reshape(own_in, n_rows, 2, in_cols), even_odd)
    sent = sent.astype(BF16).reshape(n_xl, n_rows // n_xl, 2, 2, groups, group, n_cols)
    sent = jnp.transpose(sent, (0, 2, 4, 3, 5, 1, 6)).reshape(n_xl, taps, half)
    sent = jnp.broadcast_to(sent[None], (n_y,) + sent.shape).reshape(n_chan, taps, half)
    sent, cotangent = lax.optimization_barrier((sent, cotangent))
    patches = swap(sent, CHAN)

    above = lax.ppermute(cotangent[:, n_rows - 1], TILE, ahead)
    below = lax.ppermute(cotangent[:, 0], TILE, back)

    mix = jnp.transpose(w_mix, (0, 1, 3, 2)).reshape(9 * own_out, all_out)
    turned = jnp.transpose(w_down.reshape(2, 2, n_y, n_xl, own_in, own_out), (2, 5, 3, 0, 1, 4))
    wide = n_xl * taps
    spare = own_out * wide // half
    turned = turned.reshape(n_y, own_out // spare, spare, wide)
    turned = jnp.transpose(turned, (0, 2, 1, 3)).reshape(n_y, 1, spare, half)
    turned = jnp.broadcast_to(turned, (n_y, n_xl, spare, half)).reshape(n_chan, spare, half)
    cols, partial = call(
        grad_hidden_kernel,
        (
            shape((9 * own_out, cells), BF16),
            shape((n_chan, pair_out + spare, half), BF16),
        ),
        2 * mix.size * cells,
        above,
        cotangent.reshape(own_out, cells),
        below,
        mix,
        turned,
    )
    patches, partial, other_down = lax.optimization_barrier((patches, partial, other_down))
    partial = swap(partial, CHAN)

    down = jnp.stack([jnp.where(first, w_down, other_down), jnp.where(first, other_down, w_down)])
    down = down.reshape(n_xl, 2, 2, n_chan, groups, group, own_out)
    down = jnp.transpose(down, (0, 6, 3, 1, 4, 2, 5)).reshape(pair_out, 4 * all_in)
    patches = patches.reshape(4 * all_in, half)
    preact = dot("dk,kq->dq", down, patches)
    cdf = normal_cdf(preact)
    slope = cdf + preact * normal_pdf(preact)
    hidden = (preact * cdf).astype(BF16)
    halo = jnp.where(first, hidden[:, :n_cols], hidden[:, half - n_cols :])
    halo = lax.ppermute(halo, ("xl",) + TILE, back + [(n_tile + i, n_tile + j) for i, j in ahead])
    (both,) = call(
        spread_kernel,
        (shape((n_chan, pair_out + pair_out * n_cols // half, half), BF16),),
        0,
        hidden,
        halo,
    )
    both, slope, partial = lax.optimization_barrier((both, slope, partial))
    both = swap(both, CHAN)
    grad_pre, down_keep, down_give = call_core(
        grad_pre_kernel,
        (
            shape((pair_out, half), BF16),
            shape((all_out, 2 * own_out), F32),
            shape((all_out, 2 * own_out), BF16),
        ),
        2 * patches.size * pair_out,
        side.reshape(1),
        partial,
        slope,
        patches,
    )
    down_more = lax.ppermute(down_give, "xl", flip)
    near = [grad_pre] + [
        lax.ppermute(grad_pre, "y", [(i, (i + k) % n_y) for i in range(n_y)])
        for k in range(1, n_y)
    ]

    rows = all_out // n_tile
    width = 12 * own_out
    core = lax.axis_index("core").reshape(1)
    keep, give = grad_mix_parts(core, both, cols, down_keep, down_more, n_tile, width)
    total = keep + lax.ppermute(give, "core", flip).astype(F32)
    total = swap(total.astype(BF16), ("z", "xh"))
    total = jnp.sum(total.astype(F32), axis=0) * scale
    grad_mix = total[:, : 9 * own_out].reshape(rows, 3, 3, own_out)
    piece = total[:, 9 * own_out : 11 * own_out].reshape(2, group, 2, own_out)
    grad_down = jnp.transpose(piece, (1, 2, 0, 3))

    (mixed,) = call(
        mixed_kernel, (shape((own_out, cells), BF16),), 2 * mix.size * cells, mix, both
    )
    mixed = mixed.reshape(own_out, n_rows, n_cols)

    turned = partial[:, pair_out:].reshape(n_chan, spare, own_out // spare, wide)
    turned = jnp.transpose(turned, (0, 2, 1, 3)).reshape(n_y, pair_out, wide)
    line = lax.axis_index("y")
    grad_image = sum(
        dot("dk,dq->kq", lax.dynamic_index_in_dim(turned, (line - k) % n_y, 0, False), near[k])
        for k in range(n_y)
    )
    grad_image = grad_image.astype(BF16).reshape(n_xl, taps, half)
    mine = jnp.where(first, grad_image[0], grad_image[1])
    theirs = lax.ppermute(jnp.where(first, grad_image[1], grad_image[0]), "xl", flip)
    grad_image = jnp.concatenate(
        [jnp.where(first, mine, theirs), jnp.where(first, theirs, mine)], axis=1
    )
    grad_image = grad_image.reshape(2, 2, own_in, n_rows, n_cols)
    grad_image = dot("abcrw,xbw->crax", grad_image, even_odd)
    grad_image = grad_image.astype(BF16).reshape(image.shape)
    return (mixed, grad_mix, grad_down, grad_image)


def solution(mesh):
    grid = mesh.devices
    n_chan, n_tile = grid.shape
    split = Mesh(grid.reshape(n_chan // 2, 2, n_tile // 4, 2, 2), CHAN + TILE)
    return jax.shard_map(
        per_device,
        mesh=split,
        in_specs=(
            P(CHAN, TILE, None),
            P(None, None, None, CHAN),
            P(None, None, None, CHAN),
            P(CHAN, TILE, None),
        ),
        out_specs=(
            P(CHAN, TILE, None),
            P(TILE, None, None, CHAN),
            P(TILE, None, None, CHAN),
            P(CHAN, TILE, None),
        ),
        check_vma=False,
    )
```
